1024 devices in a mesh: vel: 16 (over y, core), sx: 8 (over z), sy: 8 (over x).
Axes of the slice: x: 8, y: 8, z: 8, core: 2. Of those that a mesh axis runs over, the one named last changes fastest.
Arguments:
- scaled_population_table: float32 [64, 64, 32768], P('sx', 'sy', 'vel'), may hold values from 0 to 8, as said below
Outputs:
- advanced: float32 [64, 64, 32768], P('sx', 'sy', 'vel')
The draws below stay inside these ranges and needn't reach their ends.
Inputs may be any that keep to these rules, and one draw needn't show every extreme that they name: `scaled_population_table`: every entry is positive.
All inputs are finite; a program needn't handle non-finite values.
Results may differ from the reference program's by a relative error of at most 0.0003.
Values sent between devices are 32-bit elements; how exact they have to be, the bound alone decides.
A program may use at most 32 MiB of HBM per device.

```python
import math
import jax
import jax.numpy as jnp
from jax import lax

KV = 32
NV = 32768
GRID_ROWS_X = 64
GRID_ROWS_Y = 64


def draw_scaled_population_table(key, part):
    subkeys = jax.random.split(jax.random.fold_in(key, 17), 3)
    vel_index = jnp.arange(NV, dtype=jnp.int32)
    levels = (vel_index // (KV * KV), vel_index // KV % KV, vel_index % KV)
    particle_speeds = [(2 * one_level + 1 - KV).astype(jnp.float32) * (4.5 / KV) for one_level in levels]

    def population(subkey):
        sampler_seed_handle = jax.random.split(subkey, 3)
        local_matter_amount = jax.random.uniform(sampler_seed_handle[0], (GRID_ROWS_X, GRID_ROWS_Y, 1), minval=0.3, maxval=1.2)
        bulk_flow_components = jax.random.uniform(sampler_seed_handle[1], (3, GRID_ROWS_X, GRID_ROWS_Y, 1), minval=-0.8, maxval=0.8)
        kinetic_warmth_level = jnp.exp(jax.random.uniform(sampler_seed_handle[2], (GRID_ROWS_X, GRID_ROWS_Y, 1), minval=math.log(0.6), maxval=math.log(1.8)))
        velocity_dispersion_width = (particle_speeds[0] - bulk_flow_components[0]) ** 2 + (particle_speeds[1] - bulk_flow_components[1]) ** 2 + (particle_speeds[2] - bulk_flow_components[2]) ** 2
        return local_matter_amount * kinetic_warmth_level ** (-1.5) * jnp.exp(-velocity_dispersion_width / (2.0 * kinetic_warmth_level))
    mixture = population(subkeys[0]) + population(subkeys[1])
    jitter = jax.random.uniform(subkeys[2], (GRID_ROWS_X, GRID_ROWS_Y, NV), minval=-0.25, maxval=0.25)
    return (mixture * (1.0 + jitter)).astype(jnp.float32)


def setup_inputs(seed: int = 0) -> dict:
    keys = jax.random.split(jax.random.key(seed), 2)
    scaled_population_table = draw_scaled_population_table(jax.random.fold_in(keys[1], 71), 0)
    return dict(scaled_population_table=scaled_population_table)


vel_bound = 4.5
time_step = 0.25 / 4.5
baseline_collision_interval = 0.25
power_law_index = 0.81
diffusivity_ratio_coefficient = 2.0 / 3.0
highest = lax.Precision.HIGHEST


def velocity_table(vel_index):
    levels = (vel_index // (KV * KV), (vel_index // KV) % KV, vel_index % KV)
    return tuple((2 * one_level + 1 - KV).astype(jnp.float32) * (vel_bound / KV) for one_level in levels)


def quad_weight():
    return (2.0 * vel_bound / KV) ** 3 * (2.0 * math.pi) ** -1.5


def minmod(former, latter):
    return 0.5 * (jnp.sign(former) + jnp.sign(latter)) * jnp.minimum(jnp.abs(former), jnp.abs(latter))


def flux_change(padded, velocity, along_axis):
    length = padded.shape[along_axis]
    behind = lax.slice_in_dim(padded, 0, length - 2, axis=along_axis)
    middle = lax.slice_in_dim(padded, 1, length - 1, axis=along_axis)
    ahead_cell = lax.slice_in_dim(padded, 2, length, axis=along_axis)
    slopes = minmod(middle - behind, ahead_cell - middle)
    face_low = lax.slice_in_dim(middle + 0.5 * slopes, 0, length - 3, axis=along_axis)
    face_high = lax.slice_in_dim(middle - 0.5 * slopes, 1, length - 2, axis=along_axis)
    fluxes = jnp.maximum(velocity, 0.0) * face_low + jnp.minimum(velocity, 0.0) * face_high
    return lax.slice_in_dim(fluxes, 1, length - 3, axis=along_axis) - lax.slice_in_dim(fluxes, 0, length - 4, axis=along_axis)


def block_width():
    return math.gcd(NV, 2048)


def block_speeds(block_index):
    block_start = (block_index * block_width()).astype(jnp.int32)
    vel_index = block_start + jnp.arange(block_width(), dtype=jnp.int32)
    return block_start, velocity_table(vel_index)


def local_fluid_snapshot(scaled_population_table):
    blocks = NV // block_width()

    def add_bulk(block_index, running):
        block_start, particle_speeds = block_speeds(block_index)
        vel_piece = lax.dynamic_slice_in_dim(scaled_population_table, block_start, block_width(), 2)
        squares = particle_speeds[0] * particle_speeds[0] + particle_speeds[1] * particle_speeds[1] + particle_speeds[2] * particle_speeds[2]
        moment_basis = jnp.stack([jnp.ones_like(particle_speeds[0]), particle_speeds[0], particle_speeds[1], particle_speeds[2], squares])
        return running + jnp.einsum("xyv,mv->xym", vel_piece, moment_basis, precision=highest)

    integrated_sums_list = lax.fori_loop(0, blocks, add_bulk, jnp.zeros((GRID_ROWS_X, GRID_ROWS_Y, 5), jnp.float32)) * quad_weight()
    local_matter_amount = integrated_sums_list[..., 0:1]
    bulk_flow_components = tuple(integrated_sums_list[..., column:column + 1] / local_matter_amount for column in (1, 2, 3))
    bulk_flow_norm_square = bulk_flow_components[0] * bulk_flow_components[0] + bulk_flow_components[1] * bulk_flow_components[1] + bulk_flow_components[2] * bulk_flow_components[2]
    kinetic_warmth_level = (integrated_sums_list[..., 4:5] / local_matter_amount - bulk_flow_norm_square) / 3.0

    def add_heat(block_index, running):
        block_start, particle_speeds = block_speeds(block_index)
        vel_piece = lax.dynamic_slice_in_dim(scaled_population_table, block_start, block_width(), 2)
        neighbour_displacement_list = [particle_speeds[column] - bulk_flow_components[column] for column in range(3)]
        velocity_dispersion_width = neighbour_displacement_list[0] * neighbour_displacement_list[0] + neighbour_displacement_list[1] * neighbour_displacement_list[1] + neighbour_displacement_list[2] * neighbour_displacement_list[2]
        weighted = vel_piece * velocity_dispersion_width
        return running + jnp.stack([jnp.sum(weighted * neighbour_displacement_list[column], axis=2) for column in range(3)], axis=-1)

    heat_total = lax.fori_loop(0, blocks, add_heat, jnp.zeros((GRID_ROWS_X, GRID_ROWS_Y, 3), jnp.float32)) * (0.5 * quad_weight())
    energy_current_triple = tuple(heat_total[..., column:column + 1] for column in range(3))
    return local_matter_amount, bulk_flow_components, kinetic_warmth_level, energy_current_triple


def advance(scaled_population_table):
    local_matter_amount, bulk_flow_components, kinetic_warmth_level, energy_current_triple = local_fluid_snapshot(scaled_population_table)
    collision_rate_coefficient = local_matter_amount * kinetic_warmth_level ** (1.0 - power_law_index) / baseline_collision_interval

    def one_block(block_index):
        block_start, particle_speeds = block_speeds(block_index)
        vel_piece = lax.dynamic_slice_in_dim(scaled_population_table, block_start, block_width(), 2)
        padded = jnp.pad(vel_piece, ((2, 2), (2, 2), (0, 0)), mode="wrap")
        neighbour_displacement_list = [particle_speeds[column] - bulk_flow_components[column] for column in range(3)]
        velocity_dispersion_width = neighbour_displacement_list[0] * neighbour_displacement_list[0] + neighbour_displacement_list[1] * neighbour_displacement_list[1] + neighbour_displacement_list[2] * neighbour_displacement_list[2]
        gaussian_rest_profile = local_matter_amount * kinetic_warmth_level ** -1.5 * jnp.exp(-velocity_dispersion_width / (2.0 * kinetic_warmth_level))
        directional_energy_current = neighbour_displacement_list[0] * energy_current_triple[0] + neighbour_displacement_list[1] * energy_current_triple[1] + neighbour_displacement_list[2] * energy_current_triple[2]
        shakhov_attractor_profile = gaussian_rest_profile * (1.0 + (1.0 - diffusivity_ratio_coefficient) * directional_energy_current / (5.0 * local_matter_amount * kinetic_warmth_level * kinetic_warmth_level) * (velocity_dispersion_width / kinetic_warmth_level - 5.0))
        transport = flux_change(padded[:, 2:-2], particle_speeds[0], 0) + flux_change(padded[2:-2, :], particle_speeds[1], 1)
        return vel_piece + time_step * (collision_rate_coefficient * (shakhov_attractor_profile - vel_piece) - transport)

    stacked = lax.map(one_block, jnp.arange(NV // block_width(), dtype=jnp.int32))
    return jnp.moveaxis(stacked, 0, 2).reshape(GRID_ROWS_X, GRID_ROWS_Y, NV)


def reference(scaled_population_table):
    sectioned = advance(scaled_population_table)
    return 0.5 * scaled_population_table + 0.5 * advance(sectioned)
```

```python
import functools

import jax
import jax.numpy as jnp
from jax import lax
from jax.experimental import pallas as pl
from jax.experimental.pallas import tpu as pltpu
from jax.sharding import PartitionSpec as P

KV = 32
BOUND = 4.5
DT = 0.25 / 4.5
UNIT = BOUND / KV
WEIGHT = (2.0 * BOUND / KV) ** 3 * (2.0 * 3.141592653589793) ** (-1.5)
MESH = pl.DeviceIdType.MESH
HIGHEST = lax.Precision.HIGHEST
NC = 64
LANES = 128


def functional_table():
    index = lax.broadcasted_iota(jnp.int32, (8, 1024), 1)
    row = lax.broadcasted_iota(jnp.int32, (8, 1024), 0)
    b = (2 * (index // KV) + 1 - KV).astype(jnp.float32) * UNIT
    e = (2 * (index % KV) + 1 - KV).astype(jnp.float32) * UNIT
    one = jnp.ones_like(b)
    rest = b * b + e * e
    rows = (one, b, e, b * b, b * e, e * e, b * rest, e * rest)
    table = jnp.zeros_like(b)
    for position, value in enumerate(rows):
        table = jnp.where(row == position, value, table)
    return table * WEIGHT


def partial_sums(cells, table):
    halves = [
        lax.dot_general(
            table,
            cells[:, half * 1024 : (half + 1) * 1024],
            (((1,), (1,)), ((), ())),
            precision=HIGHEST,
            preferred_element_type=jnp.float32,
        )
        for half in range(2)
    ]
    return jnp.concatenate(halves, axis=1)


def cell_coefficients(sums_ref, n_vel):
    lane = lax.broadcasted_iota(jnp.int32, (8, LANES), 1)
    second = (lane >= NC).astype(jnp.float32)
    powers = [None] * 4
    for source in range(n_vel):
        level = (4 * source + 1 - KV) * UNIT + second * (2.0 * UNIT)
        term = sums_ref[source]
        for power in range(4):
            powers[power] = term if powers[power] is None else powers[power] + term
            term = term * level
    r0, r1, r2, r3 = (value + pltpu.roll(value, NC, 1) for value in powers)
    n = r0[0:1]
    ma, mb, me = r1[0:1], r0[1:2], r0[2:3]
    aa, ab, ae, bb, be, ee = r2[0:1], r1[1:2], r1[2:3], r0[3:4], r0[4:5], r0[5:6]
    ta = r3[0:1] + r1[3:4] + r1[5:6]
    tb = r2[1:2] + r0[6:7]
    te = r2[2:3] + r0[7:8]
    inv_n = 1.0 / n
    ua, ub, ue = ma * inv_n, mb * inv_n, me * inv_n
    energy = aa + bb + ee
    speed2 = ua * ua + ub * ub + ue * ue
    temp = (energy * inv_n - speed2) * (1.0 / 3.0)
    common = 2.0 * n * speed2 - energy
    qa = 0.5 * (ta - 2.0 * (ua * aa + ub * ab + ue * ae) + ua * common)
    qb = 0.5 * (tb - 2.0 * (ua * ab + ub * bb + ue * be) + ub * common)
    qe = 0.5 * (te - 2.0 * (ua * ae + ub * be + ue * ee) + ue * common)
    log_t = jnp.log(temp)
    inv_t = 1.0 / temp
    dt_rate = n * jnp.exp(0.19 * log_t) * (DT / 0.25)
    amp = dt_rate * n * jnp.exp(-1.5 * log_t)
    scale = (1.0 - 2.0 / 3.0) / 5.0 * inv_n * inv_t * inv_t
    return ua, ub, ue, inv_t, amp, 1.0 - dt_rate, qa * scale, qb * scale, qe * scale


def write_coefficients(sums_ref, rows_ref, coef_ref, n_vel):
    rows_ref[...] = jnp.zeros_like(rows_ref)
    for position, value in enumerate(cell_coefficients(sums_ref, n_vel)):
        rows_ref[position : position + 1, :] = value
    coef_ref[...] = rows_ref[...].T


def clamp(value, low, high):
    return jnp.minimum(jnp.maximum(value, low), high)


def upwind(behind2, behind, here, ahead):
    d = here - behind
    low, high = jnp.minimum(d, 0.0), jnp.maximum(d, 0.0)
    slope = clamp(ahead, low, high)
    slope_behind = clamp(behind2, low, high)
    return d + 0.5 * (slope - slope_behind)


def advance_row(x, field, low_ref, high_ref, coef_ref, sign, speeds_a, emit):
    row = lax.broadcasted_iota(jnp.int32, (8, LANES), 0)
    lane = lax.broadcasted_iota(jnp.int32, (8, LANES), 1)
    first, last = row == 0, row == 7
    ce = (2 * (lane % KV) + 1 - KV).astype(jnp.float32) * UNIT
    lane_b = (2 * (lane // KV) - 3).astype(jnp.float32) * UNIT
    cell = coef_ref[pl.ds(pl.multiple_of(x * 8, 8), 8), :]
    ua, ub, ue, inv_t, amp, keep, qa, qb, qe = (
        jnp.broadcast_to(cell[:, c : c + 1], (8, LANES)) for c in range(9)
    )
    half_t = 0.5 * inv_t
    se = ce - ue
    se2, seq = se * se, se * qe
    level = []
    for speed in speeds_a:
        sa = speed - ua
        level.append((amp * jnp.exp(-(sa * sa) * half_t), sa * sa * inv_t - 5.0, sa * qa))
    for s in range(8):
        cb = lane_b + (8 * s - 28) * UNIT
        sb = cb - ub
        square = sb * sb + se2
        gauss = jnp.exp(-square * half_t)
        ratio = square * inv_t
        heat = sb * qb + seq
        vb = jnp.abs(cb) * DT
        for t in range(2):
            lanes = pl.ds((8 * t + s) * LANES, LANES)
            height, ratio_a, heat_a = level[t]
            relaxed = height * gauss * (1.0 + (heat + heat_a) * (ratio + ratio_a))
            g = field[x + 2, :, lanes]
            gm = field[x + 2 - sign, :, lanes]
            gmm = field[x + 2 - 2 * sign, :, lanes]
            gp = field[x + 2 + sign, :, lanes]
            along_x = upwind(gm - gmm, gm, g, gp - g)
            lo = low_ref[x, :, lanes]
            hi = high_ref[x, :, lanes]
            back = pltpu.roll(jnp.where(last, lo, g), 1, 0)
            front = pltpu.roll(jnp.where(first, hi, g), 7, 0)
            if s >= 4:
                d = g - back
                edge = lo - pltpu.roll(lo, 1, 0)
                before = pltpu.roll(jnp.where(last, edge, d), 1, 0)
                along_y = upwind(before, back, g, front - g)
            else:
                d = g - front
                edge = hi - pltpu.roll(hi, 7, 0)
                before = pltpu.roll(jnp.where(first, edge, d), 7, 0)
                along_y = upwind(before, front, g, back - g)
            speed = jnp.abs(speeds_a[t]) * DT
            emit(lanes, keep * g + relaxed - (speed * along_x + vb * along_y))


def kernel(
    n_vel, n_x, n_y, f_hbm, out_hbm,
    field, field2, low, high, low2, high2, out_v,
    send1, send2, sums1, sums2, rows, coef,
    in_sem, out_sem, halo_send, halo_recv, sum_send, sum_recv,
):
    v, sx, sy = lax.axis_index("vel"), lax.axis_index("sx"), lax.axis_index("sy")
    up_x, down_x = lax.rem(sx + 1, n_x), lax.rem(sx + n_x - 1, n_x)
    up_y, down_y = lax.rem(sy + 1, n_y), lax.rem(sy + n_y - 1, n_y)
    sides = ({"sx": up_x}, {"sx": down_x}, {"sy": up_y}, {"sy": down_y})

    barrier = pltpu.get_barrier_semaphore()
    for side in sides:
        pl.semaphore_signal(barrier, inc=1, device_id=side, device_id_type=MESH)
    for j in range(1, n_vel):
        pl.semaphore_signal(
            barrier, inc=1, device_id={"vel": lax.rem(v + j, n_vel)}, device_id_type=MESH
        )
    load = pltpu.make_async_copy(f_hbm, field.at[pl.ds(2, 8)], in_sem)
    load.start()

    table = functional_table()
    speeds_a = [
        (4 * v + 2 * t + 1 - KV).astype(jnp.float32) * UNIT for t in range(2)
    ]
    sign = jnp.where(v >= n_vel // 2, 1, -1)

    def exchange(source, low_dst, high_dst, stage):
        copies = []
        parts = (
            (source.at[pl.ds(8, 2)], source.at[pl.ds(0, 2)]),
            (source.at[pl.ds(2, 2)], source.at[pl.ds(10, 2)]),
            (source.at[pl.ds(2, 8), pl.ds(6, 2)], low_dst.at[:, pl.ds(6, 2)]),
            (source.at[pl.ds(2, 8), pl.ds(0, 2)], high_dst.at[:, pl.ds(0, 2)]),
        )
        for i, ((src, dst), side) in enumerate(zip(parts, sides)):
            copy = pltpu.make_async_remote_copy(
                src_ref=src, dst_ref=dst,
                send_sem=halo_send.at[stage, i], recv_sem=halo_recv.at[stage, i],
                device_id=side, device_id_type=MESH,
            )
            copy.start()
            copies.append(copy)
        return copies

    def share(send, sums, stage):
        copies = []
        for j in range(1, n_vel):
            copy = pltpu.make_async_remote_copy(
                src_ref=send, dst_ref=sums.at[v],
                send_sem=sum_send.at[stage, j], recv_sem=sum_recv.at[stage, v],
                device_id={"vel": lax.rem(v + j, n_vel)}, device_id_type=MESH,
            )
            copy.start()
            copies.append(copy)
        return copies

    def gather(send, sums, stage):
        for j in range(1, n_vel):
            other = lax.rem(v + j, n_vel)
            pltpu.make_async_remote_copy(
                src_ref=send, dst_ref=sums.at[other],
                send_sem=sum_send.at[stage, j], recv_sem=sum_recv.at[stage, other],
                device_id={"vel": other}, device_id_type=MESH,
            ).wait_recv()

    load.wait()
    own = partial_sums(field[pl.ds(2, 8)].reshape(NC, 2048), table)
    send1[...] = own
    sums1[v] = own
    pl.semaphore_wait(barrier, 4 + n_vel - 1)
    started = share(send1, sums1, 0)
    halos = exchange(field, low, high, 0)
    gather(send1, sums1, 0)
    write_coefficients(sums1, rows, coef, n_vel)
    for copy in halos:
        copy.wait_recv()
    started += halos

    @pl.loop(0, 8)
    def _(x):
        def emit(lanes, value):
            field2[x + 2, :, lanes] = value

        advance_row(x, field, low, high, coef, sign, speeds_a, emit)

    halos = exchange(field2, low2, high2, 1)
    own = partial_sums(field2[pl.ds(2, 8)].reshape(NC, 2048), table)
    send2[...] = own
    sums2[v] = own
    started += share(send2, sums2, 1)
    gather(send2, sums2, 1)
    write_coefficients(sums2, rows, coef, n_vel)
    for copy in halos:
        copy.wait_recv()
    started += halos

    @pl.loop(0, 8)
    def _(x):
        def emit(lanes, value):
            out_v[x, :, lanes] = 0.5 * (field[x + 2, :, lanes] + value)

        advance_row(x, field2, low2, high2, coef, sign, speeds_a, emit)

    store = pltpu.make_async_copy(out_v, out_hbm, out_sem)
    store.start()
    for copy in started:
        copy.wait_send()
    store.wait()


def solution(mesh):
    n_vel, n_x, n_y = mesh.shape["vel"], mesh.shape["sx"], mesh.shape["sy"]

    def step(table):
        block = table.shape
        return pl.pallas_call(
            functools.partial(kernel, n_vel, n_x, n_y),
            out_shape=jax.ShapeDtypeStruct(block, jnp.float32),
            in_specs=[pl.BlockSpec(memory_space=pl.ANY)],
            out_specs=pl.BlockSpec(memory_space=pl.ANY),
            scratch_shapes=[
                pltpu.VMEM((12, 8, 2048), jnp.float32),
                pltpu.VMEM((12, 8, 2048), jnp.float32),
                pltpu.VMEM(block, jnp.float32),
                pltpu.VMEM(block, jnp.float32),
                pltpu.VMEM(block, jnp.float32),
                pltpu.VMEM(block, jnp.float32),
                pltpu.VMEM(block, jnp.float32),
                pltpu.VMEM((8, LANES), jnp.float32),
                pltpu.VMEM((8, LANES), jnp.float32),
                pltpu.VMEM((n_vel, 8, LANES), jnp.float32),
                pltpu.VMEM((n_vel, 8, LANES), jnp.float32),
                pltpu.VMEM((LANES, LANES), jnp.float32),
                pltpu.VMEM((LANES, LANES), jnp.float32),
                pltpu.SemaphoreType.DMA,
                pltpu.SemaphoreType.DMA,
                pltpu.SemaphoreType.DMA((2, 4)),
                pltpu.SemaphoreType.DMA((2, 4)),
                pltpu.SemaphoreType.DMA((2, n_vel)),
                pltpu.SemaphoreType.DMA((2, n_vel)),
            ],
            compiler_params=pltpu.CompilerParams(
                collective_id=0, has_side_effects=True
            ),
        )(table)

    return jax.shard_map(
        step,
        mesh=mesh,
        in_specs=(P("sx", "sy", "vel"),),
        out_specs=P("sx", "sy", "vel"),
        check_vma=False,
    )
```

```python
import functools

import jax
import jax.numpy as jnp
from jax import lax
from jax.experimental import pallas as pl
from jax.experimental.pallas import tpu as pltpu
from jax.sharding import PartitionSpec as P

KV = 32
BOUND = 4.5
DT = 0.25 / 4.5
UNIT = BOUND / KV
WEIGHT = (2.0 * BOUND / KV) ** 3 * (2.0 * 3.141592653589793) ** (-1.5)
MESH = pl.DeviceIdType.MESH
HIGHEST = lax.Precision.HIGHEST
NC = 64
LANES = 128


def functional_table():
    index = lax.broadcasted_iota(jnp.int32, (8, 1024), 1)
    row = lax.broadcasted_iota(jnp.int32, (8, 1024), 0)
    b = (2 * (index // KV) + 1 - KV).astype(jnp.float32) * UNIT
    e = (2 * (index % KV) + 1 - KV).astype(jnp.float32) * UNIT
    one = jnp.ones_like(b)
    rest = b * b + e * e
    rows = (one, b, e, b * b, b * e, e * e, b * rest, e * rest)
    table = jnp.zeros_like(b)
    for position, value in enumerate(rows):
        table = jnp.where(row == position, value, table)
    return table * WEIGHT


def partial_sums(cells, table):
    halves = [
        lax.dot_general(
            table,
            cells[:, half * 1024 : (half + 1) * 1024],
            (((1,), (1,)), ((), ())),
            precision=HIGHEST,
            preferred_element_type=jnp.float32,
        )
        for half in range(2)
    ]
    return jnp.concatenate(halves, axis=1)


def cell_coefficients(sums_ref, n_vel):
    lane = lax.broadcasted_iota(jnp.int32, (8, LANES), 1)
    second = (lane >= NC).astype(jnp.float32)
    powers = [None] * 4
    for source in range(n_vel):
        level = (4 * source + 1 - KV) * UNIT + second * (2.0 * UNIT)
        term = sums_ref[source]
        for power in range(4):
            powers[power] = term if powers[power] is None else powers[power] + term
            term = term * level
    r0, r1, r2, r3 = (value + pltpu.roll(value, NC, 1) for value in powers)
    n = r0[0:1]
    ma, mb, me = r1[0:1], r0[1:2], r0[2:3]
    aa, ab, ae, bb, be, ee = r2[0:1], r1[1:2], r1[2:3], r0[3:4], r0[4:5], r0[5:6]
    ta = r3[0:1] + r1[3:4] + r1[5:6]
    tb = r2[1:2] + r0[6:7]
    te = r2[2:3] + r0[7:8]
    inv_n = 1.0 / n
    ua, ub, ue = ma * inv_n, mb * inv_n, me * inv_n
    energy = aa + bb + ee
    speed2 = ua * ua + ub * ub + ue * ue
    temp = (energy * inv_n - speed2) * (1.0 / 3.0)
    common = 2.0 * n * speed2 - energy
    qa = 0.5 * (ta - 2.0 * (ua * aa + ub * ab + ue * ae) + ua * common)
    qb = 0.5 * (tb - 2.0 * (ua * ab + ub * bb + ue * be) + ub * common)
    qe = 0.5 * (te - 2.0 * (ua * ae + ub * be + ue * ee) + ue * common)
    log_t = jnp.log(temp)
    inv_t = 1.0 / temp
    dt_rate = n * jnp.exp(0.19 * log_t) * (DT / 0.25)
    amp = dt_rate * n * jnp.exp(-1.5 * log_t)
    scale = (1.0 - 2.0 / 3.0) / 5.0 * inv_n * inv_t * inv_t
    return ua, ub, ue, inv_t, amp, 1.0 - dt_rate, qa * scale, qb * scale, qe * scale


def write_coefficients(sums_ref, rows_ref, coef_ref, n_vel):
    rows_ref[...] = jnp.zeros_like(rows_ref)
    for position, value in enumerate(cell_coefficients(sums_ref, n_vel)):
        rows_ref[position : position + 1, :] = value
    coef_ref[...] = rows_ref[...].T


def clamp(value, low, high):
    return jnp.minimum(jnp.maximum(value, low), high)


def upwind(behind2, behind, here, ahead):
    d = here - behind
    low, high = jnp.minimum(d, 0.0), jnp.maximum(d, 0.0)
    slope = clamp(ahead, low, high)
    slope_behind = clamp(behind2, low, high)
    return d + 0.5 * (slope - slope_behind)


def advance_row(x, field, low_ref, high_ref, coef_ref, sign, speeds_a, emit):
    row = lax.broadcasted_iota(jnp.int32, (8, LANES), 0)
    lane = lax.broadcasted_iota(jnp.int32, (8, LANES), 1)
    first, last = row == 0, row == 7
    ce = (2 * (lane % KV) + 1 - KV).astype(jnp.float32) * UNIT
    lane_b = (2 * (lane // KV) - 3).astype(jnp.float32) * UNIT
    cell = coef_ref[pl.ds(pl.multiple_of(x * 8, 8), 8), :]
    ua, ub, ue, inv_t, amp, keep, qa, qb, qe = (
        jnp.broadcast_to(cell[:, c : c + 1], (8, LANES)) for c in range(9)
    )
    half_t = 0.5 * inv_t
    se = ce - ue
    se2, seq = se * se, se * qe
    level = []
    for speed in speeds_a:
        sa = speed - ua
        level.append((amp * jnp.exp(-(sa * sa) * half_t), sa * sa * inv_t - 5.0, sa * qa))
    for s in range(8):
        cb = lane_b + (8 * s - 28) * UNIT
        sb = cb - ub
        square = sb * sb + se2
        gauss = jnp.exp(-square * half_t)
        ratio = square * inv_t
        heat = sb * qb + seq
        vb = jnp.abs(cb) * DT
        for t in range(2):
            lanes = pl.ds((8 * t + s) * LANES, LANES)
            height, ratio_a, heat_a = level[t]
            relaxed = height * gauss * (1.0 + (heat + heat_a) * (ratio + ratio_a))
            g = field[x + 2, :, lanes]
            gm = field[x + 2 - sign, :, lanes]
            gmm = field[x + 2 - 2 * sign, :, lanes]
            gp = field[x + 2 + sign, :, lanes]
            along_x = upwind(gm - gmm, gm, g, gp - g)
            lo = low_ref[x, :, lanes]
            hi = high_ref[x, :, lanes]
            back = pltpu.roll(jnp.where(last, lo, g), 1, 0)
            front = pltpu.roll(jnp.where(first, hi, g), 7, 0)
            if s >= 4:
                d = g - back
                edge = lo - pltpu.roll(lo, 1, 0)
                before = pltpu.roll(jnp.where(last, edge, d), 1, 0)
                along_y = upwind(before, back, g, front - g)
            else:
                d = g - front
                edge = hi - pltpu.roll(hi, 7, 0)
                before = pltpu.roll(jnp.where(first, edge, d), 7, 0)
                along_y = upwind(before, front, g, back - g)
            speed = jnp.abs(speeds_a[t]) * DT
            emit(lanes, keep * g + relaxed - (speed * along_x + vb * along_y))


def kernel(
    n_vel, n_x, n_y, f_hbm, out_v,
    field, field2, low, high, low2, high2, mine, sums, rows, coef, total,
    in_sem, send_sem, x_sem, y_sem, sum_sem,
):
    v, sx, sy = lax.axis_index("vel"), lax.axis_index("sx"), lax.axis_index("sy")
    up_x, down_x = lax.rem(sx + 1, n_x), lax.rem(sx + n_x - 1, n_x)
    up_y, down_y = {"sy": lax.rem(sy + 1, n_y)}, {"sy": lax.rem(sy + n_y - 1, n_y)}
    upward = v >= n_vel // 2
    sign = jnp.where(upward, 1, -1)
    order = sorted(range(1, n_vel), key=lambda j: -min(j, n_vel - j))
    others = [{"vel": lax.rem(v + j, n_vel)} for j in order]

    load = pltpu.make_async_copy(f_hbm, field.at[pl.ds(2, 8)], in_sem)
    load.start()
    barrier = pltpu.get_barrier_semaphore()
    near = others + [{"sx": up_x}, {"sx": down_x}, up_y, down_y]
    for side in near:
        pl.semaphore_signal(barrier, inc=1, device_id=side, device_id_type=MESH)

    table = functional_table()
    speeds_a = [
        (4 * v + 2 * t + 1 - KV).astype(jnp.float32) * UNIT for t in range(2)
    ]

    def send(src, dst, recv_sem, to):
        pltpu.make_async_remote_copy(
            src_ref=src, dst_ref=dst, send_sem=send_sem, recv_sem=recv_sem,
            device_id=to, device_id_type=MESH,
        ).start()

    def wait(ref, sem):
        pltpu.make_async_copy(ref, ref, sem).wait()

    def exchange_x(source, stage):
        upwind_to = {"sx": jnp.where(upward, up_x, down_x)}
        other_to = {"sx": jnp.where(upward, down_x, up_x)}
        parts = (
            (jnp.where(upward, 8, 2), jnp.where(upward, 0, 10), 2, upwind_to),
            (jnp.where(upward, 2, 9), jnp.where(upward, 10, 1), 1, other_to),
        )
        for src, dst, size, to in parts:
            send(source.at[pl.ds(src, size)], source.at[pl.ds(dst, size)], x_sem.at[stage], to)

    def exchange_y(source, low_dst, high_dst, stage):
        for t in range(2):
            for positive in range(2):
                lanes = pl.ds(1024 * t + 512 * positive, 512)
                row, size = (6, 2) if positive else (7, 1)
                send(
                    source.at[pl.ds(2, 8), pl.ds(row, size), lanes],
                    low_dst.at[:, pl.ds(row, size), lanes], y_sem.at[stage], up_y,
                )
                size = 1 if positive else 2
                send(
                    source.at[pl.ds(2, 8), pl.ds(0, size), lanes],
                    high_dst.at[:, pl.ds(0, size), lanes], y_sem.at[stage], down_y,
                )

    def own_sums(source, stage):
        value = partial_sums(source[pl.ds(2, 8)].reshape(NC, 2048), table)
        mine[stage] = value
        sums[stage, v] = value

    def share(stage):
        for to in others:
            send(mine.at[stage], sums.at[stage, v], sum_sem.at[stage], to)

    def gather(stage):
        wait(total.at[pl.ds(0, n_vel - 1)], sum_sem.at[stage])
        write_coefficients(sums.at[stage], rows, coef, n_vel)

    def arrive_x(stage):
        wait(total.at[pl.ds(0, 3 * 16)], x_sem.at[stage])

    def arrive_y(stage):
        wait(total.at[pl.ds(0, 3 * 16)], y_sem.at[stage])

    def row_of(i):
        return jnp.where(upward, i, 7 - i)

    load.wait()
    own_sums(field, 0)
    pl.semaphore_wait(barrier, len(near))
    share(0)
    exchange_x(field, 0)
    exchange_y(field, low, high, 0)
    arrive_x(0)
    arrive_y(0)
    gather(0)

    def first_step(i):
        x = row_of(i)

        def emit(lanes, value):
            field2[x + 2, :, lanes] = value

        advance_row(x, field, low, high, coef, sign, speeds_a, emit)

    @pl.loop(0, 3)
    def _(i):
        first_step(lax.rem(i + 6, 8))

    exchange_x(field2, 1)

    @pl.loop(1, 6)
    def _(i):
        first_step(i)

    exchange_y(field2, low2, high2, 1)
    own_sums(field2, 1)
    share(1)

    def second_step(i):
        x = row_of(i)

        def emit(lanes, value):
            out_v[x, :, lanes] = 0.5 * (field[x + 2, :, lanes] + value)

        advance_row(x, field2, low2, high2, coef, sign, speeds_a, emit)

    arrive_y(1)
    gather(1)

    @pl.loop(2, 7)
    def _(i):
        second_step(i)

    arrive_x(1)

    @pl.loop(0, 3)
    def _(i):
        second_step(lax.rem(i + 7, 8))

    wait(total, send_sem)


def solution(mesh):
    n_vel, n_x, n_y = mesh.shape["vel"], mesh.shape["sx"], mesh.shape["sy"]

    def step(table):
        block = table.shape
        table = pltpu.with_memory_space_constraint(table, pltpu.HBM)
        return pl.pallas_call(
            functools.partial(kernel, n_vel, n_x, n_y),
            out_shape=jax.ShapeDtypeStruct(block, jnp.float32),
            in_specs=[pl.BlockSpec(memory_space=pltpu.HBM)],
            out_specs=pl.BlockSpec(memory_space=pltpu.VMEM),
            scratch_shapes=[
                pltpu.VMEM((12, 8, 2048), jnp.float32),
                pltpu.VMEM((12, 8, 2048), jnp.float32),
                pltpu.VMEM(block, jnp.float32),
                pltpu.VMEM(block, jnp.float32),
                pltpu.VMEM(block, jnp.float32),
                pltpu.VMEM(block, jnp.float32),
                pltpu.VMEM((2, 8, LANES), jnp.float32),
                pltpu.VMEM((2, n_vel, 8, LANES), jnp.float32),
                pltpu.VMEM((LANES, LANES), jnp.float32),
                pltpu.VMEM((LANES, LANES), jnp.float32),
                pltpu.VMEM((2 * (6 * 16 + n_vel - 1), 8, LANES), jnp.float32),
                pltpu.SemaphoreType.DMA,
                pltpu.SemaphoreType.DMA,
                pltpu.SemaphoreType.DMA((2,)),
                pltpu.SemaphoreType.DMA((2,)),
                pltpu.SemaphoreType.DMA((2,)),
            ],
            compiler_params=pltpu.CompilerParams(
                collective_id=0,
                has_side_effects=True,
                vmem_limit_bytes=16 * 1024 * 1024,
            ),
        )(table)

    return jax.shard_map(
        step,
        mesh=mesh,
        in_specs=(P("sx", "sy", "vel"),),
        out_specs=P("sx", "sy", "vel"),
        check_vma=False,
    )
```

```python
import functools

import jax
import jax.numpy as jnp
from jax import lax
from jax.experimental import pallas as pl
from jax.experimental.pallas import tpu as pltpu
from jax.sharding import PartitionSpec as P

KV = 32
BOUND = 4.5
DT = 0.25 / 4.5
UNIT = BOUND / KV
WEIGHT = (2.0 * BOUND / KV) ** 3 * (2.0 * 3.141592653589793) ** (-1.5)
MESH = pl.DeviceIdType.MESH
HIGHEST = lax.Precision.HIGHEST
NC = 64
LANES = 128


def functional_table():
    index = lax.broadcasted_iota(jnp.int32, (8, 1024), 1)
    row = lax.broadcasted_iota(jnp.int32, (8, 1024), 0)
    b = (2 * (index // KV) + 1 - KV).astype(jnp.float32) * UNIT
    e = (2 * (index % KV) + 1 - KV).astype(jnp.float32) * UNIT
    one = jnp.ones_like(b)
    rest = b * b + e * e
    rows = (one, b, e, b * b, b * e, e * e, b * rest, e * rest)
    table = jnp.zeros_like(b)
    for position, value in enumerate(rows):
        table = jnp.where(row == position, value, table)
    return table * WEIGHT


def partial_sums(cells, table, first):
    pieces = []
    size = cells.shape[0]
    for half in range(2):
        value = lax.dot_general(
            table,
            cells[:, half * 1024 : (half + 1) * 1024],
            (((1,), (1,)), ((), ())),
            precision=HIGHEST,
            preferred_element_type=jnp.float32,
        )
        before, after = first, NC - first - size
        if before:
            pieces.append(jnp.zeros((8, before), jnp.float32))
        pieces.append(value)
        if after:
            pieces.append(jnp.zeros((8, after), jnp.float32))
    return jnp.concatenate(pieces, axis=1)


def cell_coefficients(sums_ref, n_vel):
    lane = lax.broadcasted_iota(jnp.int32, (8, LANES), 1)
    second = (lane >= NC).astype(jnp.float32)
    powers = [None] * 4
    for source in range(n_vel):
        level = (4 * source + 1 - KV) * UNIT + second * (2.0 * UNIT)
        term = sums_ref[source]
        for power in range(4):
            powers[power] = term if powers[power] is None else powers[power] + term
            term = term * level
    r0, r1, r2, r3 = (value + pltpu.roll(value, NC, 1) for value in powers)
    n = r0[0:1]
    ma, mb, me = r1[0:1], r0[1:2], r0[2:3]
    aa, ab, ae, bb, be, ee = r2[0:1], r1[1:2], r1[2:3], r0[3:4], r0[4:5], r0[5:6]
    ta = r3[0:1] + r1[3:4] + r1[5:6]
    tb = r2[1:2] + r0[6:7]
    te = r2[2:3] + r0[7:8]
    inv_n = 1.0 / n
    ua, ub, ue = ma * inv_n, mb * inv_n, me * inv_n
    energy = aa + bb + ee
    speed2 = ua * ua + ub * ub + ue * ue
    temp = (energy * inv_n - speed2) * (1.0 / 3.0)
    common = 2.0 * n * speed2 - energy
    qa = 0.5 * (ta - 2.0 * (ua * aa + ub * ab + ue * ae) + ua * common)
    qb = 0.5 * (tb - 2.0 * (ua * ab + ub * bb + ue * be) + ub * common)
    qe = 0.5 * (te - 2.0 * (ua * ae + ub * be + ue * ee) + ue * common)
    log_t = jnp.log(temp)
    inv_t = 1.0 / temp
    dt_rate = n * jnp.exp(0.19 * log_t) * (DT / 0.25)
    amp = dt_rate * n * jnp.exp(-1.5 * log_t)
    scale = (1.0 - 2.0 / 3.0) / 5.0 * inv_n * inv_t * inv_t
    return ua, ub, ue, inv_t, amp, 1.0 - dt_rate, qa * scale, qb * scale, qe * scale


def write_coefficients(sums_ref, rows_ref, coef_ref, n_vel):
    rows_ref[...] = jnp.zeros_like(rows_ref)
    for position, value in enumerate(cell_coefficients(sums_ref, n_vel)):
        rows_ref[position : position + 1, :] = value
    coef_ref[...] = rows_ref[...].T


def clamp(value, low, high):
    return jnp.minimum(jnp.maximum(value, low), high)


def upwind(behind2, behind, here, ahead):
    d = here - behind
    low, high = jnp.minimum(d, 0.0), jnp.maximum(d, 0.0)
    slope = clamp(ahead, low, high)
    slope_behind = clamp(behind2, low, high)
    return d + 0.5 * (slope - slope_behind)


def advance_row(x, field, low_ref, high_ref, coef_ref, sign, speeds_a, emit):
    row = lax.broadcasted_iota(jnp.int32, (8, LANES), 0)
    lane = lax.broadcasted_iota(jnp.int32, (8, LANES), 1)
    first, last = row == 0, row == 7
    ce = (2 * (lane % KV) + 1 - KV).astype(jnp.float32) * UNIT
    lane_b = (2 * (lane // KV) - 3).astype(jnp.float32) * UNIT
    cell = coef_ref[pl.ds(pl.multiple_of(x * 8, 8), 8), :]
    ua, ub, ue, inv_t, amp, keep, qa, qb, qe = (
        jnp.broadcast_to(cell[:, c : c + 1], (8, LANES)) for c in range(9)
    )
    half_t = 0.5 * inv_t
    se = ce - ue
    se2, seq = se * se, se * qe
    level = []
    for speed in speeds_a:
        sa = speed - ua
        level.append((amp * jnp.exp(-(sa * sa) * half_t), sa * sa * inv_t - 5.0, sa * qa))
    for s in range(8):
        cb = lane_b + (8 * s - 28) * UNIT
        sb = cb - ub
        square = sb * sb + se2
        gauss = jnp.exp(-square * half_t)
        ratio = square * inv_t
        heat = sb * qb + seq
        vb = jnp.abs(cb) * DT
        for t in range(2):
            lanes = pl.ds((8 * t + s) * LANES, LANES)
            height, ratio_a, heat_a = level[t]
            relaxed = height * gauss * (1.0 + (heat + heat_a) * (ratio + ratio_a))
            g = field[x + 2, :, lanes]
            gm = field[x + 2 - sign, :, lanes]
            gmm = field[x + 2 - 2 * sign, :, lanes]
            gp = field[x + 2 + sign, :, lanes]
            along_x = upwind(gm - gmm, gm, g, gp - g)
            lo = low_ref[x, :, lanes]
            hi = high_ref[x, :, lanes]
            back = pltpu.roll(jnp.where(last, lo, g), 1, 0)
            front = pltpu.roll(jnp.where(first, hi, g), 7, 0)
            if s >= 4:
                d = g - back
                edge = lo - pltpu.roll(lo, 1, 0)
                before = pltpu.roll(jnp.where(last, edge, d), 1, 0)
                along_y = upwind(before, back, g, front - g)
            else:
                d = g - front
                edge = hi - pltpu.roll(hi, 7, 0)
                before = pltpu.roll(jnp.where(first, edge, d), 7, 0)
                along_y = upwind(before, front, g, back - g)
            speed = jnp.abs(speeds_a[t]) * DT
            emit(lanes, keep * g + relaxed - (speed * along_x + vb * along_y))


def kernel(
    n_vel, n_x, n_y, f_hbm, out_v,
    field, field2, low, high, low2, high2, mine, sums, rows, coef, total,
    in_sem, send_sem, x_sem, y_sem, sum_sem, go,
):
    v, sx, sy = lax.axis_index("vel"), lax.axis_index("sx"), lax.axis_index("sy")
    up_x, down_x = {"sx": lax.rem(sx + 1, n_x)}, {"sx": lax.rem(sx + n_x - 1, n_x)}
    up_y, down_y = {"sy": lax.rem(sy + 1, n_y)}, {"sy": lax.rem(sy + n_y - 1, n_y)}
    upward = v >= n_vel // 2
    downward = v < n_vel // 2
    sign = jnp.where(upward, 1, -1)

    def fold(i, n):
        return jnp.where(i < n // 2, i, n + n // 2 - 1 - i)

    corner = jnp.logical_and(sx == 0, sy == 0)
    top = jnp.logical_and(corner, v == 0)

    def rank_of(vel):
        plain = 2 * fold(vel // 2, n_vel // 2) + 1 - lax.rem(vel, 2)
        in_corner = jnp.where(vel == 0, n_vel - 1, plain - jnp.where(plain > 1, 1, 0))
        return jnp.where(corner, in_corner, plain)

    def side_above(side, plain):
        there_x, there_y = side.get("sx", sx), side.get("sy", sy)
        there = jnp.logical_and(jnp.logical_and(there_x == 0, there_y == 0), v == 0)
        return jnp.logical_and(jnp.logical_or(plain, there), jnp.logical_not(top))

    y_rank = fold(sy, n_y)
    sides = tuple(
        (side, side_above(side, plain), index)
        for side, plain, index in (
            (up_x, up_x["sx"] > sx, 1),
            (down_x, down_x["sx"] > sx, 0),
            (up_y, fold(up_y["sy"], n_y) > y_rank, 3),
            (down_y, fold(down_y["sy"], n_y) > y_rank, 2),
        )
    )
    higher = [above for _, above, _ in sides]
    lower = [jnp.logical_not(above) for above in higher]
    rank = rank_of(v)
    order = sorted(range(1, n_vel), key=lambda j: -min(j, n_vel - j))
    others = [{"vel": lax.rem(v + j, n_vel)} for j in order]

    barrier = pltpu.get_barrier_semaphore()
    for to, above, _ in sides:
        @pl.when(above)
        def _(to=to):
            pl.semaphore_signal(barrier, inc=1, device_id=to, device_id_type=MESH)

    for to in others:
        @pl.when(rank_of(to["vel"]) > rank)
        def _(to=to):
            pl.semaphore_signal(barrier, inc=1, device_id=to, device_id_type=MESH)

    load = pltpu.make_async_copy(f_hbm, field.at[pl.ds(2, 8)], in_sem)
    load.start()

    table = functional_table()
    speeds_a = [
        (4 * v + 2 * t + 1 - KV).astype(jnp.float32) * UNIT for t in range(2)
    ]

    def send(src, dst, recv_sem, to):
        pltpu.make_async_remote_copy(
            src_ref=src, dst_ref=dst, send_sem=send_sem, recv_sem=recv_sem,
            device_id=to, device_id_type=MESH,
        ).start()

    def wait(tiles, sem):
        pltpu.make_async_copy(
            total.at[pl.ds(0, tiles)], total.at[pl.ds(0, tiles)], sem
        ).wait()

    def send_x(source, stage, rising):
        to, sem = (up_x, x_sem.at[stage, 0]) if rising else (down_x, x_sem.at[stage, 1])
        far, near = ((8, 0), (9, 1)) if rising else ((2, 10), (2, 10))

        @pl.when(upward if rising else downward)
        def _():
            src, dst = far
            send(source.at[pl.ds(src, 2)], source.at[pl.ds(dst, 2)], sem, to)

        @pl.when(downward if rising else upward)
        def _():
            src, dst = near
            send(source.at[pl.ds(src, 1)], source.at[pl.ds(dst, 1)], sem, to)

    def arrive_x(stage, rising):
        sem = x_sem.at[stage, 0 if rising else 1]

        @pl.when(upward if rising else downward)
        def _():
            wait(2 * 16, sem)

        @pl.when(downward if rising else upward)
        def _():
            wait(16, sem)

    def send_y(source, dst, sem, start, count, rising):
        for t in range(2):
            for positive in range(2):
                lanes = pl.ds(1024 * t + 512 * positive, 512)
                if rising:
                    row, size = (6, 2) if positive else (7, 1)
                else:
                    row, size = 0, (1 if positive else 2)
                send(
                    source.at[pl.ds(2 + start, count), pl.ds(row, size), lanes],
                    dst.at[pl.ds(start, count), pl.ds(row, size), lanes],
                    sem, up_y if rising else down_y,
                )

    def exchange_y(source, low_dst, high_dst, sem, start, count):
        send_y(source, low_dst, sem, start, count, True)
        send_y(source, high_dst, sem, start, count, False)

    def own_sums(source, slot, start, count):
        cells = source[pl.ds(2 + start, count)].reshape(8 * count, 2048)
        value = partial_sums(cells, table, 8 * start)
        mine[slot] = value
        sums[slot, v] = value

    def share(slot):
        for to in others:
            send(mine.at[slot], sums.at[slot, v], sum_sem.at[slot], to)

    def gather(slot):
        wait(n_vel - 1, sum_sem.at[slot])
        write_coefficients(sums.at[slot], rows, coef, n_vel)

    def first_step(x):
        def emit(lanes, value):
            field2[x + 2, :, lanes] = value

        advance_row(x, field, low, high, coef, sign, speeds_a, emit)

    def second_step(x):
        def emit(lanes, value):
            out_v[x, :, lanes] = 0.5 * (field[x + 2, :, lanes] + value)

        advance_row(x, field2, low2, high2, coef, sign, speeds_a, emit)

    begin = (
        lambda: send_x(field, 0, True),
        lambda: send_x(field, 0, False),
        lambda: send_y(field, low, y_sem.at[0], 0, 8, True),
        lambda: send_y(field, high, y_sem.at[0], 0, 8, False),
    )
    entered = sum(below.astype(jnp.int32) for below in lower) + rank

    @pl.when(entered > 0)
    def _():
        pl.semaphore_wait(barrier, entered)

    for (to, _, index), below in zip(sides, lower):
        @pl.when(below)
        def _(to=to, index=index):
            pl.semaphore_signal(go.at[index], inc=1, device_id=to, device_id_type=MESH)

    for to in others:
        @pl.when(rank_of(to["vel"]) < rank)
        def _(to=to):
            pl.semaphore_signal(go.at[4], inc=1, device_id=to, device_id_type=MESH)

    load.wait()
    for start, below in zip(begin, lower):
        pl.when(below)(start)

    own_sums(field, 0, 0, 8)
    for to in others:
        @pl.when(rank_of(to["vel"]) < rank)
        def _(to=to):
            send(mine.at[0], sums.at[0, v], sum_sem.at[0], to)

    def begin_above(index):
        @pl.when(higher[index])
        def _():
            pl.semaphore_wait(go.at[index], 1)
            begin[index]()

    begin_above(2)
    begin_above(3)
    begin_above(0)

    @pl.when(rank < n_vel - 1)
    def _():
        pl.semaphore_wait(go.at[4], n_vel - 1 - rank)

    for to in others:
        @pl.when(rank_of(to["vel"]) > rank)
        def _(to=to):
            send(mine.at[0], sums.at[0, v], sum_sem.at[0], to)

    wait(3 * 16, y_sem.at[0])
    gather(0)

    @pl.loop(2, 6)
    def _(x):
        first_step(x)

    begin_above(1)
    arrive_x(0, False)

    @pl.loop(6, 8)
    def _(x):
        first_step(x)

    send_x(field2, 1, True)
    own_sums(field2, 1, 2, 6)
    share(1)
    exchange_y(field2, low2, high2, y_sem.at[1], 2, 6)
    arrive_x(0, True)

    @pl.loop(0, 2)
    def _(x):
        first_step(x)

    own_sums(field2, 2, 0, 2)
    share(2)
    send_x(field2, 1, False)
    exchange_y(field2, low2, high2, y_sem.at[2], 0, 2)

    wait(36, y_sem.at[1])
    arrive_x(1, False)
    gather(1)

    @pl.loop(2, 8)
    def _(x):
        second_step(x)

    wait(12, y_sem.at[2])
    arrive_x(1, True)
    gather(2)

    @pl.loop(0, 2)
    def _(x):
        second_step(x)

    wait(2 * 6 * 16 + 3 * (n_vel - 1), send_sem)


def solution(mesh):
    n_vel, n_x, n_y = mesh.shape["vel"], mesh.shape["sx"], mesh.shape["sy"]

    def step(table):
        block = table.shape
        table = pltpu.with_memory_space_constraint(table, pltpu.HBM)
        return pl.pallas_call(
            functools.partial(kernel, n_vel, n_x, n_y),
            out_shape=jax.ShapeDtypeStruct(block, jnp.float32),
            in_specs=[pl.BlockSpec(memory_space=pltpu.HBM)],
            out_specs=pl.BlockSpec(memory_space=pltpu.VMEM),
            scratch_shapes=[
                pltpu.VMEM((12, 8, 2048), jnp.float32),
                pltpu.VMEM((12, 8, 2048), jnp.float32),
                pltpu.VMEM(block, jnp.float32),
                pltpu.VMEM(block, jnp.float32),
                pltpu.VMEM(block, jnp.float32),
                pltpu.VMEM(block, jnp.float32),
                pltpu.VMEM((3, 8, LANES), jnp.float32),
                pltpu.VMEM((3, n_vel, 8, LANES), jnp.float32),
                pltpu.VMEM((LANES, LANES), jnp.float32),
                pltpu.VMEM((LANES, LANES), jnp.float32),
                pltpu.VMEM((2 * 6 * 16 + 3 * (n_vel - 1), 8, LANES), jnp.float32),
                pltpu.SemaphoreType.DMA,
                pltpu.SemaphoreType.DMA,
                pltpu.SemaphoreType.DMA((2, 2)),
                pltpu.SemaphoreType.DMA((3,)),
                pltpu.SemaphoreType.DMA((3,)),
                pltpu.SemaphoreType.REGULAR((5,)),
            ],
            compiler_params=pltpu.CompilerParams(
                collective_id=0,
                has_side_effects=True,
                vmem_limit_bytes=16 * 1024 * 1024,
            ),
        )(table)

    return jax.shard_map(
        step,
        mesh=mesh,
        in_specs=(P("sx", "sy", "vel"),),
        out_specs=P("sx", "sy", "vel"),
        check_vma=False,
    )
```

```python
import functools

import jax
import jax.numpy as jnp
from jax import lax
from jax.experimental import pallas as pl
from jax.experimental.pallas import tpu as pltpu
from jax.sharding import PartitionSpec as P

KV = 32
BOUND = 4.5
DT = 0.25 / 4.5
UNIT = BOUND / KV
WEIGHT = (2.0 * BOUND / KV) ** 3 * (2.0 * 3.141592653589793) ** (-1.5)
MESH = pl.DeviceIdType.MESH
NC = 64
LANES = 128


def functional_table():
    index = lax.broadcasted_iota(jnp.int32, (8, 1024), 1)
    row = lax.broadcasted_iota(jnp.int32, (8, 1024), 0)
    b = (2 * (index // KV) + 1 - KV).astype(jnp.float32)
    e = (2 * (index % KV) + 1 - KV).astype(jnp.float32)
    rest = b * b + e * e
    rows = (jnp.ones_like(b), b, e, b * b, b * e, e * e, b * rest, e * rest)
    table = jnp.zeros_like(b)
    for position, value in enumerate(rows):
        table = jnp.where(row == position, value, table)
    high = table.astype(jnp.bfloat16)
    low = (table - high.astype(jnp.float32)).astype(jnp.bfloat16)
    return jnp.concatenate([high, low], axis=0)


def partial_sums(cells, table, first):
    pieces = []
    size = cells.shape[0]
    for half in range(2):
        rest = cells[:, half * 1024 : (half + 1) * 1024]
        value = jnp.zeros((16, size), jnp.float32)
        for part in range(3):
            piece = rest.astype(jnp.bfloat16)
            value = value + lax.dot_general(
                table, piece, (((1,), (1,)), ((), ())),
                preferred_element_type=jnp.float32,
            )
            if part < 2:
                rest = rest - piece.astype(jnp.float32)
        before, after = first, NC - first - size
        if before:
            pieces.append(jnp.zeros((8, before), jnp.float32))
        pieces.append(value[:8] + value[8:])
        if after:
            pieces.append(jnp.zeros((8, after), jnp.float32))
    row = lax.broadcasted_iota(jnp.int32, (8, LANES), 0)
    scale = jnp.where(row == 0, 1.0, jnp.where(row < 3, UNIT, jnp.where(row < 6, UNIT**2, UNIT**3)))
    return jnp.concatenate(pieces, axis=1) * (scale * WEIGHT)


def cell_coefficients(sums_ref, n_vel):
    lane = lax.broadcasted_iota(jnp.int32, (8, LANES), 1)
    second = (lane >= NC).astype(jnp.float32)
    powers = [None] * 4
    for source in range(n_vel):
        level = (4 * source + 1 - KV) * UNIT + second * (2.0 * UNIT)
        term = sums_ref[source]
        for power in range(4):
            powers[power] = term if powers[power] is None else powers[power] + term
            term = term * level
    r0, r1, r2, r3 = (value + pltpu.roll(value, NC, 1) for value in powers)
    n = r0[0:1]
    ma, mb, me = r1[0:1], r0[1:2], r0[2:3]
    aa, ab, ae, bb, be, ee = r2[0:1], r1[1:2], r1[2:3], r0[3:4], r0[4:5], r0[5:6]
    ta = r3[0:1] + r1[3:4] + r1[5:6]
    tb = r2[1:2] + r0[6:7]
    te = r2[2:3] + r0[7:8]
    inv_n = 1.0 / n
    ua, ub, ue = ma * inv_n, mb * inv_n, me * inv_n
    energy = aa + bb + ee
    speed2 = ua * ua + ub * ub + ue * ue
    temp = (energy * inv_n - speed2) * (1.0 / 3.0)
    common = 2.0 * n * speed2 - energy
    qa = 0.5 * (ta - 2.0 * (ua * aa + ub * ab + ue * ae) + ua * common)
    qb = 0.5 * (tb - 2.0 * (ua * ab + ub * bb + ue * be) + ub * common)
    qe = 0.5 * (te - 2.0 * (ua * ae + ub * be + ue * ee) + ue * common)
    log_t = jnp.log(temp)
    inv_t = 1.0 / temp
    dt_rate = n * jnp.exp(0.19 * log_t) * (DT / 0.25)
    amp = dt_rate * n * jnp.exp(-1.5 * log_t)
    scale = (1.0 - 2.0 / 3.0) / 5.0 * inv_n * inv_t * inv_t
    return ua, ub, ue, inv_t, amp, 1.0 - dt_rate, qa * scale, qb * scale, qe * scale


def write_coefficients(sums_ref, rows_ref, coef_ref, n_vel):
    rows_ref[...] = jnp.zeros_like(rows_ref)
    for position, value in enumerate(cell_coefficients(sums_ref, n_vel)):
        rows_ref[position : position + 1, :] = value
    coef_ref[...] = rows_ref[...].T


def clamp(value, low, high):
    return jnp.minimum(jnp.maximum(value, low), high)


def upwind(behind2, behind, here, ahead):
    d = here - behind
    low, high = jnp.minimum(d, 0.0), jnp.maximum(d, 0.0)
    slope = clamp(ahead, low, high)
    slope_behind = clamp(behind2, low, high)
    return d + 0.5 * (slope - slope_behind)


def transport_tile(x, lanes, s, t, field, low_ref, high_ref, sign, speeds_a, along):
    row = lax.broadcasted_iota(jnp.int32, (8, LANES), 0)
    lane = lax.broadcasted_iota(jnp.int32, (8, LANES), 1)
    first, last = row == 0, row == 7
    g = field[x + 2, :, lanes]
    total = None
    if "x" in along:
        gm = field[x + 2 - sign, :, lanes]
        gmm = field[x + 2 - 2 * sign, :, lanes]
        gp = field[x + 2 + sign, :, lanes]
        total = jnp.abs(speeds_a[t]) * DT * upwind(gm - gmm, gm, g, gp - g)
    if "y" in along:
        lo = low_ref[x, :, lanes]
        hi = high_ref[x, :, lanes]
        back = pltpu.roll(jnp.where(last, lo, g), 1, 0)
        front = pltpu.roll(jnp.where(first, hi, g), 7, 0)
        if s >= 4:
            d = g - back
            edge = lo - pltpu.roll(lo, 1, 0)
            before = pltpu.roll(jnp.where(last, edge, d), 1, 0)
            along_y = upwind(before, back, g, front - g)
        else:
            d = g - front
            edge = hi - pltpu.roll(hi, 7, 0)
            before = pltpu.roll(jnp.where(first, edge, d), 7, 0)
            along_y = upwind(before, front, g, back - g)
        cb = (2 * (lane // KV) - 3 + 8 * s - 28).astype(jnp.float32) * UNIT
        part = jnp.abs(cb) * DT * along_y
        total = part if total is None else total + part
    return total


def transport_row(x, field, low_ref, high_ref, sign, speeds_a, along, emit):
    for s in range(8):
        for t in range(2):
            lanes = pl.ds((8 * t + s) * LANES, LANES)
            emit(lanes, transport_tile(x, lanes, s, t, field, low_ref, high_ref, sign, speeds_a, along))


def advance_row(x, field, coef_ref, speeds_a, transport, emit):
    lane = lax.broadcasted_iota(jnp.int32, (8, LANES), 1)
    ce = (2 * (lane % KV) + 1 - KV).astype(jnp.float32) * UNIT
    lane_b = (2 * (lane // KV) - 3).astype(jnp.float32) * UNIT
    cell = coef_ref[pl.ds(pl.multiple_of(x * 8, 8), 8), :]
    ua, ub, ue, inv_t, amp, keep, qa, qb, qe = (
        jnp.broadcast_to(cell[:, c : c + 1], (8, LANES)) for c in range(9)
    )
    half_t = 0.5 * inv_t
    se = ce - ue
    se2, seq = se * se, se * qe
    level = []
    for speed in speeds_a:
        sa = speed - ua
        level.append((amp * jnp.exp(-(sa * sa) * half_t), sa * sa * inv_t - 5.0, sa * qa))
    for s in range(8):
        cb = lane_b + (8 * s - 28) * UNIT
        sb = cb - ub
        square = sb * sb + se2
        gauss = jnp.exp(-square * half_t)
        ratio = square * inv_t
        heat = sb * qb + seq
        for t in range(2):
            lanes = pl.ds((8 * t + s) * LANES, LANES)
            height, ratio_a, heat_a = level[t]
            relaxed = height * gauss * (1.0 + (heat + heat_a) * (ratio + ratio_a))
            g = field[x + 2, :, lanes]
            emit(lanes, keep * g + relaxed - transport(lanes, s, t))


def kernel(
    n_vel, n_x, n_y, f_hbm, out_v,
    field, field2, low, high, low2, high2, mine, sums, rows, coef, total,
    in_sem, send_sem, x_sem, y_sem, sum_sem, go,
):
    v, sx, sy = lax.axis_index("vel"), lax.axis_index("sx"), lax.axis_index("sy")
    up_x, down_x = {"sx": lax.rem(sx + 1, n_x)}, {"sx": lax.rem(sx + n_x - 1, n_x)}
    up_y, down_y = {"sy": lax.rem(sy + 1, n_y)}, {"sy": lax.rem(sy + n_y - 1, n_y)}
    upward = v >= n_vel // 2
    downward = v < n_vel // 2
    sign = jnp.where(upward, 1, -1)

    def fold(i, n):
        return jnp.where(i < n // 2, i, n + n // 2 - 1 - i)

    corner = jnp.logical_and(sx == 0, sy == 0)
    top = jnp.logical_and(corner, v == 0)

    def rank_of(vel):
        plain = 2 * (vel // 2) + 1 - lax.rem(vel, 2)
        in_corner = jnp.where(vel == 0, n_vel - 1, plain - jnp.where(plain > 1, 1, 0))
        return jnp.where(corner, in_corner, plain)

    def side_above(side, plain):
        there_x, there_y = side.get("sx", sx), side.get("sy", sy)
        wrap = jnp.abs(there_x - sx) == n_x - 1
        there = jnp.logical_and(jnp.logical_and(there_x == 0, there_y == 0), v == 0)
        moved = jnp.logical_and(jnp.logical_or(plain, there), jnp.logical_not(top))
        return jnp.where(wrap, plain, moved)

    y_rank = fold(sy, n_y)
    sides = tuple(
        (side, side_above(side, plain), index)
        for side, plain, index in (
            (up_x, up_x["sx"] > sx, 1),
            (down_x, down_x["sx"] > sx, 0),
            (up_y, fold(up_y["sy"], n_y) > y_rank, 3),
            (down_y, fold(down_y["sy"], n_y) > y_rank, 2),
        )
    )
    higher = [above for _, above, _ in sides]
    lower = [jnp.logical_not(above) for above in higher]
    rank = rank_of(v)
    order = sorted(range(1, n_vel), key=lambda j: -min(j, n_vel - j))
    others = [{"vel": lax.rem(v + j, n_vel)} for j in order]

    load = pltpu.make_async_copy(f_hbm, field.at[pl.ds(2, 8)], in_sem)
    load.start()
    barrier = pltpu.get_barrier_semaphore()
    for to, above, _ in sides:
        @pl.when(above)
        def _(to=to):
            pl.semaphore_signal(barrier, inc=1, device_id=to, device_id_type=MESH)

    for to in others:
        @pl.when(rank_of(to["vel"]) > rank)
        def _(to=to):
            pl.semaphore_signal(barrier, inc=1, device_id=to, device_id_type=MESH)

    table = functional_table()
    speeds_a = [
        (4 * v + 2 * t + 1 - KV).astype(jnp.float32) * UNIT for t in range(2)
    ]

    def send(src, dst, recv_sem, to):
        pltpu.make_async_remote_copy(
            src_ref=src, dst_ref=dst, send_sem=send_sem, recv_sem=recv_sem,
            device_id=to, device_id_type=MESH,
        ).start()

    def wait(tiles, sem):
        pltpu.make_async_copy(
            total.at[pl.ds(0, tiles)], total.at[pl.ds(0, tiles)], sem
        ).wait()

    def send_x(source, dest, stage, rising):
        base = 2 if source is dest else 0
        to, sem = (up_x, x_sem.at[stage, 0]) if rising else (down_x, x_sem.at[stage, 1])
        far, near = ((6, 0), (7, 1)) if rising else ((0, 10), (0, 10))

        @pl.when(upward if rising else downward)
        def _():
            src, dst = far
            send(source.at[pl.ds(src + base, 2)], dest.at[pl.ds(dst, 2)], sem, to)

        @pl.when(downward if rising else upward)
        def _():
            src, dst = near
            send(source.at[pl.ds(src + base, 1)], dest.at[pl.ds(dst, 1)], sem, to)

    def arrive_x(stage, rising):
        sem = x_sem.at[stage, 0 if rising else 1]

        @pl.when(upward if rising else downward)
        def _():
            wait(2 * 16, sem)

        @pl.when(downward if rising else upward)
        def _():
            wait(16, sem)

    def send_y(source, dst, sem, start, count, rising):
        for t in range(2):
            for positive in range(2):
                lanes = pl.ds(1024 * t + 512 * positive, 512)
                if rising:
                    row, size = (6, 2) if positive else (7, 1)
                else:
                    row, size = 0, (1 if positive else 2)
                send(
                    source.at[pl.ds(2 + start, count), pl.ds(row, size), lanes],
                    dst.at[pl.ds(start, count), pl.ds(row, size), lanes],
                    sem, up_y if rising else down_y,
                )

    def exchange_y(source, low_dst, high_dst, sem, start, count):
        send_y(source, low_dst, sem, start, count, True)
        send_y(source, high_dst, sem, start, count, False)

    def own_sums(source, slot, start, count):
        cells = source[pl.ds(2 + start, count)].reshape(8 * count, 2048)
        value = partial_sums(cells, table, 8 * start)
        mine[slot] = value
        sums[slot, v] = value

    def share(slot):
        for to in others:
            send(mine.at[slot], sums.at[slot, v], sum_sem.at[slot], to)

    def gather(slot):
        wait(n_vel - 1, sum_sem.at[slot])
        write_coefficients(sums.at[slot], rows, coef, n_vel)

    def tiles(x, along, second):
        source, below, above = (field2, low2, high2) if second else (field, low, high)

        def transport(lanes, s, t):
            return transport_tile(x, lanes, s, t, source, below, above, sign, speeds_a, along)

        return transport

    def first_transport(x):
        def emit(lanes, value):
            field2[x + 2, :, lanes] = value

        transport_row(x, field, low, high, sign, speeds_a, "xy", emit)

    def first_step(x, along="xy"):
        def emit(lanes, value):
            field2[x + 2, :, lanes] = value

        def kept(lanes, s, t):
            return field2[x + 2, :, lanes]

        transport = tiles(x, along, False) if along else kept
        advance_row(x, field, coef, speeds_a, transport, emit)

    def first_step_along_x(x):
        def emit(lanes, value):
            field2[x + 2, :, lanes] = field2[x + 2, :, lanes] - value

        transport_row(x, field, low, high, sign, speeds_a, "x", emit)

    def finish(x, transport):
        def emit(lanes, value):
            out_v[x, :, lanes] = 0.5 * (field[x + 2, :, lanes] + value)

        advance_row(x, field2, coef, speeds_a, transport, emit)

    def finish_along_x(x):
        def emit(lanes, value):
            out_v[x, :, lanes] = out_v[x, :, lanes] - 0.5 * value

        transport_row(x, field2, low2, high2, sign, speeds_a, "x", emit)

    def second_transport(x):
        def emit(lanes, value):
            out_v[x, :, lanes] = value

        transport_row(x, field2, low2, high2, sign, speeds_a, "xy", emit)

    begin = (
        lambda: send_x(f_hbm, field, 0, True),
        lambda: send_x(f_hbm, field, 0, False),
        lambda: send_y(field, low, y_sem.at[0], 0, 8, True),
        lambda: send_y(field, high, y_sem.at[0], 0, 8, False),
    )
    entered = sum(below.astype(jnp.int32) for below in lower) + rank

    @pl.when(entered > 0)
    def _():
        pl.semaphore_wait(barrier, entered)

    for start, below in zip(begin[:2], lower[:2]):
        pl.when(below)(start)

    for (to, _, index), below in zip(sides, lower):
        @pl.when(below)
        def _(to=to, index=index):
            pl.semaphore_signal(go.at[index], inc=1, device_id=to, device_id_type=MESH)

    for to in others:
        @pl.when(rank_of(to["vel"]) < rank)
        def _(to=to):
            pl.semaphore_signal(go.at[4], inc=1, device_id=to, device_id_type=MESH)

    load.wait()
    for start, below in zip(begin[2:], lower[2:]):
        pl.when(below)(start)

    own_sums(field, 0, 0, 8)
    for to in others:
        @pl.when(rank_of(to["vel"]) < rank)
        def _(to=to):
            send(mine.at[0], sums.at[0, v], sum_sem.at[0], to)

    def begin_above(index):
        @pl.when(higher[index])
        def _():
            pl.semaphore_wait(go.at[index], 1)
            begin[index]()

    begin_above(2)
    begin_above(3)
    begin_above(0)

    @pl.when(rank < n_vel - 1)
    def _():
        pl.semaphore_wait(go.at[4], n_vel - 1 - rank)

    for to in others:
        @pl.when(rank_of(to["vel"]) > rank)
        def _(to=to):
            send(mine.at[0], sums.at[0, v], sum_sem.at[0], to)

    begin_above(1)
    wait(3 * 16, y_sem.at[0])
    arrive_x(0, False)

    @pl.loop(6, 8)
    def _(x):
        first_transport(x)

    gather(0)

    @pl.loop(6, 8)
    def _(x):
        first_step(x, None)

    send_x(field2, field2, 1, True)

    @pl.loop(2, 6)
    def _(x):
        first_step(x)

    own_sums(field2, 1, 2, 6)
    share(1)
    exchange_y(field2, low2, high2, y_sem.at[1], 2, 6)

    @pl.loop(0, 2)
    def _(x):
        first_step(x, "y")

    arrive_x(0, True)

    @pl.loop(0, 2)
    def _(x):
        first_step_along_x(x)

    own_sums(field2, 2, 0, 2)
    share(2)
    send_x(field2, field2, 1, False)
    exchange_y(field2, low2, high2, y_sem.at[2], 0, 2)

    wait(36, y_sem.at[1])
    arrive_x(1, False)
    gather(1)

    @pl.loop(2, 8)
    def _(x):
        finish(x, tiles(x, "xy", True))

    wait(12, y_sem.at[2])

    @pl.when(upward)
    def _():
        gather(2)

        @pl.loop(0, 2)
        def _(x):
            finish(x, tiles(x, "y", True))

        arrive_x(1, True)

        @pl.loop(0, 2)
        def _(x):
            finish_along_x(x)

    @pl.when(downward)
    def _():
        arrive_x(1, True)

        @pl.loop(0, 2)
        def _(x):
            second_transport(x)

        gather(2)

        @pl.loop(0, 2)
        def _(x):
            finish(x, lambda lanes, s, t: out_v[x, :, lanes])

    wait(2 * 6 * 16 + 3 * (n_vel - 1), send_sem)


def solution(mesh):
    n_vel, n_x, n_y = mesh.shape["vel"], mesh.shape["sx"], mesh.shape["sy"]

    def step(table):
        block = table.shape
        table = pltpu.with_memory_space_constraint(table, pltpu.HBM)
        return pl.pallas_call(
            functools.partial(kernel, n_vel, n_x, n_y),
            out_shape=jax.ShapeDtypeStruct(block, jnp.float32),
            in_specs=[pl.BlockSpec(memory_space=pltpu.HBM)],
            out_specs=pl.BlockSpec(memory_space=pltpu.VMEM),
            scratch_shapes=[
                pltpu.VMEM((12, 8, 2048), jnp.float32),
                pltpu.VMEM((12, 8, 2048), jnp.float32),
                pltpu.VMEM(block, jnp.float32),
                pltpu.VMEM(block, jnp.float32),
                pltpu.VMEM(block, jnp.float32),
                pltpu.VMEM(block, jnp.float32),
                pltpu.VMEM((3, 8, LANES), jnp.float32),
                pltpu.VMEM((3, n_vel, 8, LANES), jnp.float32),
                pltpu.VMEM((LANES, LANES), jnp.float32),
                pltpu.VMEM((LANES, LANES), jnp.float32),
                pltpu.VMEM((2 * 6 * 16 + 3 * (n_vel - 1), 8, LANES), jnp.float32),
                pltpu.SemaphoreType.DMA,
                pltpu.SemaphoreType.DMA,
                pltpu.SemaphoreType.DMA((2, 2)),
                pltpu.SemaphoreType.DMA((3,)),
                pltpu.SemaphoreType.DMA((3,)),
                pltpu.SemaphoreType.REGULAR((5,)),
            ],
            compiler_params=pltpu.CompilerParams(
                collective_id=0,
                has_side_effects=True,
                vmem_limit_bytes=16 * 1024 * 1024,
            ),
        )(table)

    return jax.shard_map(
        step,
        mesh=mesh,
        in_specs=(P("sx", "sy", "vel"),),
        out_specs=P("sx", "sy", "vel"),
        check_vma=False,
    )
```

```python
import functools

import jax
import jax.numpy as jnp
from jax import lax
from jax.experimental import pallas as pl
from jax.experimental.pallas import tpu as pltpu
from jax.sharding import PartitionSpec as P

KV = 32
BOUND = 4.5
DT = 0.25 / 4.5
UNIT = BOUND / KV
WEIGHT = (2.0 * BOUND / KV) ** 3 * (2.0 * 3.141592653589793) ** (-1.5)
MESH = pl.DeviceIdType.MESH
NC = 64
LANES = 128


def functional_table():
    index = lax.broadcasted_iota(jnp.int32, (8, 1024), 1)
    row = lax.broadcasted_iota(jnp.int32, (8, 1024), 0)
    b = (2 * (index // KV) + 1 - KV).astype(jnp.float32)
    e = (2 * (index % KV) + 1 - KV).astype(jnp.float32)
    rest = b * b + e * e
    rows = (jnp.ones_like(b), b, e, b * b, b * e, e * e, b * rest, e * rest)
    table = jnp.zeros_like(b)
    for position, value in enumerate(rows):
        table = jnp.where(row == position, value, table)
    high = table.astype(jnp.bfloat16)
    low = (table - high.astype(jnp.float32)).astype(jnp.bfloat16)
    return jnp.concatenate([high, low], axis=0)


def partial_sums(cells, table, first):
    pieces = []
    size = cells.shape[0]
    for half in range(2):
        rest = cells[:, half * 1024 : (half + 1) * 1024]
        value = jnp.zeros((16, size), jnp.float32)
        for part in range(3):
            piece = rest.astype(jnp.bfloat16)
            value = value + lax.dot_general(
                table, piece, (((1,), (1,)), ((), ())),
                preferred_element_type=jnp.float32,
            )
            if part < 2:
                rest = rest - piece.astype(jnp.float32)
        before, after = first, NC - first - size
        if before:
            pieces.append(jnp.zeros((8, before), jnp.float32))
        pieces.append(value[:8] + value[8:])
        if after:
            pieces.append(jnp.zeros((8, after), jnp.float32))
    row = lax.broadcasted_iota(jnp.int32, (8, LANES), 0)
    scale = jnp.where(row == 0, 1.0, jnp.where(row < 3, UNIT, jnp.where(row < 6, UNIT**2, UNIT**3)))
    return jnp.concatenate(pieces, axis=1) * (scale * WEIGHT)


def cell_coefficients(sums_ref, n_vel):
    lane = lax.broadcasted_iota(jnp.int32, (8, LANES), 1)
    second = (lane >= NC).astype(jnp.float32)
    powers = [None] * 4
    for source in range(n_vel):
        level = (4 * source + 1 - KV) * UNIT + second * (2.0 * UNIT)
        term = sums_ref[source]
        for power in range(4):
            powers[power] = term if powers[power] is None else powers[power] + term
            term = term * level
    r0, r1, r2, r3 = (value + pltpu.roll(value, NC, 1) for value in powers)
    n = r0[0:1]
    ma, mb, me = r1[0:1], r0[1:2], r0[2:3]
    aa, ab, ae, bb, be, ee = r2[0:1], r1[1:2], r1[2:3], r0[3:4], r0[4:5], r0[5:6]
    ta = r3[0:1] + r1[3:4] + r1[5:6]
    tb = r2[1:2] + r0[6:7]
    te = r2[2:3] + r0[7:8]
    inv_n = 1.0 / n
    ua, ub, ue = ma * inv_n, mb * inv_n, me * inv_n
    energy = aa + bb + ee
    speed2 = ua * ua + ub * ub + ue * ue
    temp = (energy * inv_n - speed2) * (1.0 / 3.0)
    common = 2.0 * n * speed2 - energy
    qa = 0.5 * (ta - 2.0 * (ua * aa + ub * ab + ue * ae) + ua * common)
    qb = 0.5 * (tb - 2.0 * (ua * ab + ub * bb + ue * be) + ub * common)
    qe = 0.5 * (te - 2.0 * (ua * ae + ub * be + ue * ee) + ue * common)
    log_t = jnp.log(temp)
    inv_t = 1.0 / temp
    dt_rate = n * jnp.exp(0.19 * log_t) * (DT / 0.25)
    amp = dt_rate * n * jnp.exp(-1.5 * log_t)
    scale = (1.0 - 2.0 / 3.0) / 5.0 * inv_n * inv_t * inv_t
    return ua, ub, ue, inv_t, amp, 1.0 - dt_rate, qa * scale, qb * scale, qe * scale


def write_coefficients(sums_ref, rows_ref, coef_ref, n_vel):
    rows_ref[...] = jnp.zeros_like(rows_ref)
    for position, value in enumerate(cell_coefficients(sums_ref, n_vel)):
        rows_ref[position : position + 1, :] = value
    coef_ref[...] = rows_ref[...].T


def clamp(value, low, high):
    return jnp.minimum(jnp.maximum(value, low), high)


def upwind(behind2, behind, here, ahead):
    d = here - behind
    low, high = jnp.minimum(d, 0.0), jnp.maximum(d, 0.0)
    slope = clamp(ahead, low, high)
    slope_behind = clamp(behind2, low, high)
    return d + 0.5 * (slope - slope_behind)


def transport_tile(x, lanes, s, t, field, low_ref, high_ref, sign, speeds_a, along):
    row = lax.broadcasted_iota(jnp.int32, (8, LANES), 0)
    lane = lax.broadcasted_iota(jnp.int32, (8, LANES), 1)
    first, last = row == 0, row == 7
    g = field[x + 2, :, lanes]
    total = None
    if "x" in along:
        gm = field[x + 2 - sign, :, lanes]
        gmm = field[x + 2 - 2 * sign, :, lanes]
        gp = field[x + 2 + sign, :, lanes]
        total = jnp.abs(speeds_a[t]) * DT * upwind(gm - gmm, gm, g, gp - g)
    if "y" in along:
        lo = low_ref[x, :, lanes]
        hi = high_ref[x, :, lanes]
        back = pltpu.roll(jnp.where(last, lo, g), 1, 0)
        front = pltpu.roll(jnp.where(first, hi, g), 7, 0)
        if s >= 4:
            d = g - back
            edge = lo - pltpu.roll(lo, 1, 0)
            before = pltpu.roll(jnp.where(last, edge, d), 1, 0)
            along_y = upwind(before, back, g, front - g)
        else:
            d = g - front
            edge = hi - pltpu.roll(hi, 7, 0)
            before = pltpu.roll(jnp.where(first, edge, d), 7, 0)
            along_y = upwind(before, front, g, back - g)
        cb = (2 * (lane // KV) - 3 + 8 * s - 28).astype(jnp.float32) * UNIT
        part = jnp.abs(cb) * DT * along_y
        total = part if total is None else total + part
    return total


def transport_row(x, field, low_ref, high_ref, sign, speeds_a, along, emit):
    for s in range(8):
        for t in range(2):
            lanes = pl.ds((8 * t + s) * LANES, LANES)
            emit(lanes, transport_tile(x, lanes, s, t, field, low_ref, high_ref, sign, speeds_a, along))


def advance_row(x, field, coef_ref, speeds_a, transport, emit, shift=2):
    lane = lax.broadcasted_iota(jnp.int32, (8, LANES), 1)
    ce = (2 * (lane % KV) + 1 - KV).astype(jnp.float32) * UNIT
    lane_b = (2 * (lane // KV) - 3).astype(jnp.float32) * UNIT
    cell = coef_ref[pl.ds(pl.multiple_of(x * 8, 8), 8), :]
    ua, ub, ue, inv_t, amp, keep, qa, qb, qe = (
        jnp.broadcast_to(cell[:, c : c + 1], (8, LANES)) for c in range(9)
    )
    half_t = 0.5 * inv_t
    se = ce - ue
    se2, seq = se * se, se * qe
    level = []
    for speed in speeds_a:
        sa = speed - ua
        level.append((amp * jnp.exp(-(sa * sa) * half_t), sa * sa * inv_t - 5.0, sa * qa))
    for s in range(8):
        cb = lane_b + (8 * s - 28) * UNIT
        sb = cb - ub
        square = sb * sb + se2
        gauss = jnp.exp(-square * half_t)
        ratio = square * inv_t
        heat = sb * qb + seq
        for t in range(2):
            lanes = pl.ds((8 * t + s) * LANES, LANES)
            height, ratio_a, heat_a = level[t]
            relaxed = height * gauss * (1.0 + (heat + heat_a) * (ratio + ratio_a))
            g = field[x + shift, :, lanes]
            emit(lanes, keep * g + relaxed - transport(lanes, s, t))


def kernel(
    n_vel, n_x, n_y, f_hbm, out_v, edge_rows, edge_coef,
    field, field2, low, high, low2, high2, mine, sums, rows, coef, total,
    in_sem, send_sem, x_sem, y_sem, sum_sem, go,
):
    v, sx, sy = lax.axis_index("vel"), lax.axis_index("sx"), lax.axis_index("sy")
    up_x, down_x = {"sx": lax.rem(sx + 1, n_x)}, {"sx": lax.rem(sx + n_x - 1, n_x)}
    up_y, down_y = {"sy": lax.rem(sy + 1, n_y)}, {"sy": lax.rem(sy + n_y - 1, n_y)}
    upward = v >= n_vel // 2
    downward = v < n_vel // 2
    sign = jnp.where(upward, 1, -1)

    def fold(i, n):
        return jnp.where(i < n // 2, i, n + n // 2 - 1 - i)

    corner = jnp.logical_and(sx == 0, sy == 0)
    top = jnp.logical_and(corner, v == 0)

    def rank_of(vel):
        plain = vel + 1 - 2 * lax.rem(vel, 2)
        in_corner = jnp.where(vel == 0, n_vel - 1, plain - jnp.where(plain > 1, 1, 0))
        return jnp.where(corner, in_corner, plain)

    def side_above(side, plain):
        there_x, there_y = side.get("sx", sx), side.get("sy", sy)
        wrap = jnp.abs(there_x - sx) == n_x - 1
        there = jnp.logical_and(jnp.logical_and(there_x == 0, there_y == 0), v == 0)
        moved = jnp.logical_and(jnp.logical_or(plain, there), jnp.logical_not(top))
        return jnp.where(wrap, plain, moved)

    y_rank = fold(sy, n_y)
    sides = tuple(
        (side, side_above(side, plain), index)
        for side, plain, index in (
            (up_x, up_x["sx"] > sx, 1),
            (down_x, down_x["sx"] > sx, 0),
            (up_y, fold(up_y["sy"], n_y) > y_rank, 3),
            (down_y, fold(down_y["sy"], n_y) > y_rank, 2),
        )
    )
    higher = [above for _, above, _ in sides]
    lower = [jnp.logical_not(above) for above in higher]
    rank = rank_of(v)
    order = sorted(range(1, n_vel), key=lambda j: -min(j, n_vel - j))
    others = [{"vel": lax.rem(v + j, n_vel)} for j in order]
    other_above = [rank_of(to["vel"]) > rank for to in others]
    other_below = [jnp.logical_not(above) for above in other_above]

    load = pltpu.make_async_copy(f_hbm, field.at[pl.ds(2, 8)], in_sem)
    load.start()
    barrier = pltpu.get_barrier_semaphore()
    for to, above, _ in sides:
        @pl.when(above)
        def _(to=to):
            pl.semaphore_signal(barrier, inc=1, device_id=to, device_id_type=MESH)

    for to, above in zip(others, other_above):
        @pl.when(above)
        def _(to=to):
            pl.semaphore_signal(barrier, inc=1, device_id=to, device_id_type=MESH)

    table = functional_table()
    speeds_a = [
        (4 * v + 2 * t + 1 - KV).astype(jnp.float32) * UNIT for t in range(2)
    ]

    def send(src, dst, recv_sem, to):
        pltpu.make_async_remote_copy(
            src_ref=src, dst_ref=dst, send_sem=send_sem, recv_sem=recv_sem,
            device_id=to, device_id_type=MESH,
        ).start()

    def wait(tiles, sem):
        pltpu.make_async_copy(
            total.at[pl.ds(0, tiles)], total.at[pl.ds(0, tiles)], sem
        ).wait()

    def send_x(source, dest, stage, rising):
        base = 2 if source is dest else 0
        to, sem = (up_x, x_sem.at[stage, 0]) if rising else (down_x, x_sem.at[stage, 1])
        far, near = ((6, 0), (7, 1)) if rising else ((0, 10), (0, 10))

        @pl.when(upward if rising else downward)
        def _():
            src, dst = far
            send(source.at[pl.ds(src + base, 2)], dest.at[pl.ds(dst, 2)], sem, to)

        @pl.when(downward if rising else upward)
        def _():
            src, dst = near
            send(source.at[pl.ds(src + base, 1)], dest.at[pl.ds(dst, 1)], sem, to)

    def arrive_x(stage, rising):
        sem = x_sem.at[stage, 0 if rising else 1]

        @pl.when(upward if rising else downward)
        def _():
            wait(2 * 16, sem)

        @pl.when(downward if rising else upward)
        def _():
            wait(16, sem)

    def send_y(source, dst, sem, start, count, rising):
        for t in range(2):
            for positive in range(2):
                lanes = pl.ds(1024 * t + 512 * positive, 512)
                if rising:
                    row, size = (6, 2) if positive else (7, 1)
                else:
                    row, size = 0, (1 if positive else 2)
                send(
                    source.at[pl.ds(2 + start, count), pl.ds(row, size), lanes],
                    dst.at[pl.ds(start, count), pl.ds(row, size), lanes],
                    sem, up_y if rising else down_y,
                )

    def exchange_y(source, low_dst, high_dst, sem, start, count):
        send_y(source, low_dst, sem, start, count, True)
        send_y(source, high_dst, sem, start, count, False)

    def own_sums(source, slot, start, count):
        cells = source[pl.ds(2 + start, count)].reshape(8 * count, 2048)
        value = partial_sums(cells, table, 8 * start)
        mine[slot] = value
        sums[slot, v] = value

    def share(slot):
        for to in others:
            send(mine.at[slot], sums.at[slot, v], sum_sem.at[slot], to)

    def gather(slot):
        wait(n_vel - 1, sum_sem.at[slot])
        write_coefficients(sums.at[slot], rows, edge_coef if slot == 2 else coef, n_vel)

    def tiles(x, along, second):
        source, below, above = (field2, low2, high2) if second else (field, low, high)

        def transport(lanes, s, t):
            return transport_tile(x, lanes, s, t, source, below, above, sign, speeds_a, along)

        return transport

    def first_transport(x):
        def emit(lanes, value):
            field2[x + 2, :, lanes] = value

        transport_row(x, field, low, high, sign, speeds_a, "xy", emit)

    def first_step(x, along="xy"):
        def emit(lanes, value):
            field2[x + 2, :, lanes] = value

        def kept(lanes, s, t):
            return field2[x + 2, :, lanes]

        transport = tiles(x, along, False) if along else kept
        advance_row(x, field, coef, speeds_a, transport, emit)

    def first_step_along_x(x):
        def emit(lanes, value):
            field2[x + 2, :, lanes] = field2[x + 2, :, lanes] - value

        transport_row(x, field, low, high, sign, speeds_a, "x", emit)

    def finish(x, transport):
        def emit(lanes, value):
            out_v[x, :, lanes] = 0.5 * (field[x + 2, :, lanes] + value)

        advance_row(x, field2, coef, speeds_a, transport, emit)

    def add_along_x(x):
        def emit(lanes, value):
            out_v[x, :, lanes] = out_v[x, :, lanes] + value

        transport_row(x, field2, low2, high2, sign, speeds_a, "x", emit)

    def second_transport(x, along):
        def emit(lanes, value):
            out_v[x, :, lanes] = value

        transport_row(x, field2, low2, high2, sign, speeds_a, along, emit)

    begin = (
        lambda: send_x(f_hbm, field, 0, True),
        lambda: send_x(f_hbm, field, 0, False),
        lambda: send_y(field, low, y_sem.at[0], 0, 8, True),
        lambda: send_y(field, high, y_sem.at[0], 0, 8, False),
    )
    entered = sum(below.astype(jnp.int32) for below in lower) + rank

    @pl.when(entered > 0)
    def _():
        pl.semaphore_wait(barrier, entered)

    for start, below in zip(begin[:2], lower[:2]):
        pl.when(below)(start)

    for (to, _, index), below in zip(sides, lower):
        @pl.when(below)
        def _(to=to, index=index):
            pl.semaphore_signal(go.at[index], inc=1, device_id=to, device_id_type=MESH)

    for to, below in zip(others, other_below):
        @pl.when(below)
        def _(to=to):
            pl.semaphore_signal(go.at[4], inc=1, device_id=to, device_id_type=MESH)

    load.wait()
    for start, below in zip(begin[2:], lower[2:]):
        pl.when(below)(start)

    own_sums(field, 0, 0, 8)
    for to, below in zip(others, other_below):
        @pl.when(below)
        def _(to=to):
            send(mine.at[0], sums.at[0, v], sum_sem.at[0], to)

    def begin_above(index):
        @pl.when(higher[index])
        def _():
            pl.semaphore_wait(go.at[index], 1)
            begin[index]()

    begin_above(2)
    begin_above(3)
    begin_above(0)

    @pl.when(rank < n_vel - 1)
    def _():
        pl.semaphore_wait(go.at[4], n_vel - 1 - rank)

    for to, above in zip(others, other_above):
        @pl.when(above)
        def _(to=to):
            send(mine.at[0], sums.at[0, v], sum_sem.at[0], to)

    begin_above(1)
    wait(3 * 16, y_sem.at[0])
    arrive_x(0, False)

    @pl.loop(6, 8)
    def _(x):
        first_transport(x)

    gather(0)

    @pl.loop(6, 8)
    def _(x):
        first_step(x, None)

    send_x(field2, field2, 1, True)

    @pl.loop(2, 6)
    def _(x):
        first_step(x)

    own_sums(field2, 1, 2, 6)
    share(1)
    exchange_y(field2, low2, high2, y_sem.at[1], 2, 6)

    @pl.loop(0, 2)
    def _(x):
        first_step(x, "y")

    arrive_x(0, True)

    @pl.loop(0, 2)
    def _(x):
        first_step_along_x(x)

    own_sums(field2, 2, 0, 2)
    share(2)
    send_x(field2, field2, 1, False)
    exchange_y(field2, low2, high2, y_sem.at[2], 0, 2)

    wait(36, y_sem.at[1])
    arrive_x(1, False)
    gather(1)

    @pl.loop(2, 8)
    def _(x):
        finish(x, tiles(x, "xy", True))

    wait(12, y_sem.at[2])

    @pl.loop(0, 2)
    def _(x):
        edge_rows[x] = field2[x + 2]
        edge_rows[x + 2] = field[x + 2]

    @pl.when(upward)
    def _():
        @pl.loop(0, 2)
        def _(x):
            second_transport(x, "y")

        gather(2)
        arrive_x(1, True)

        @pl.loop(0, 2)
        def _(x):
            add_along_x(x)

    @pl.when(downward)
    def _():
        arrive_x(1, True)

        @pl.loop(0, 2)
        def _(x):
            second_transport(x, "xy")

        gather(2)

    for t in range(2):
        edge_coef[pl.ds(NC + 8 * t, 8), :] = jnp.full((8, LANES), speeds_a[t])

    wait(2 * 6 * 16 + 3 * (n_vel - 1), send_sem)


def finish_kernel(value, edge_rows, edge_coef, out_hbm, done, sem):
    rest = pltpu.make_async_copy(value.at[pl.ds(2, 6)], out_hbm.at[pl.ds(2, 6)], sem.at[0])
    rest.start()
    speeds_a = [edge_coef[NC + 8 * t : NC + 8 * t + 8, :] for t in range(2)]
    for x in range(2):
        def emit(lanes, new):
            done[x, :, lanes] = 0.5 * (edge_rows[x + 2, :, lanes] + new)

        advance_row(
            x, edge_rows, edge_coef, speeds_a,
            lambda lanes, s, t: value[x, :, lanes], emit, 0,
        )
    last = pltpu.make_async_copy(done, out_hbm.at[pl.ds(0, 2)], sem.at[1])
    last.start()
    last.wait()
    rest.wait()


def solution(mesh):
    n_vel, n_x, n_y = mesh.shape["vel"], mesh.shape["sx"], mesh.shape["sy"]

    def step(table):
        block = table.shape
        table = pltpu.with_memory_space_constraint(table, pltpu.HBM)
        parts = pl.pallas_call(
            functools.partial(kernel, n_vel, n_x, n_y),
            out_shape=[
                jax.ShapeDtypeStruct(block, jnp.float32),
                jax.ShapeDtypeStruct((4, 8, 2048), jnp.float32),
                jax.ShapeDtypeStruct((LANES, LANES), jnp.float32),
            ],
            in_specs=[pl.BlockSpec(memory_space=pltpu.HBM)],
            out_specs=[pl.BlockSpec(memory_space=pltpu.VMEM)] * 3,
            scratch_shapes=[
                pltpu.VMEM((12, 8, 2048), jnp.float32),
                pltpu.VMEM((12, 8, 2048), jnp.float32),
                pltpu.VMEM(block, jnp.float32),
                pltpu.VMEM(block, jnp.float32),
                pltpu.VMEM(block, jnp.float32),
                pltpu.VMEM(block, jnp.float32),
                pltpu.VMEM((3, 8, LANES), jnp.float32),
                pltpu.VMEM((3, n_vel, 8, LANES), jnp.float32),
                pltpu.VMEM((LANES, LANES), jnp.float32),
                pltpu.VMEM((LANES, LANES), jnp.float32),
                pltpu.VMEM((2 * 6 * 16 + 3 * (n_vel - 1), 8, LANES), jnp.float32),
                pltpu.SemaphoreType.DMA,
                pltpu.SemaphoreType.DMA,
                pltpu.SemaphoreType.DMA((2, 2)),
                pltpu.SemaphoreType.DMA((3,)),
                pltpu.SemaphoreType.DMA((3,)),
                pltpu.SemaphoreType.REGULAR((5,)),
            ],
            compiler_params=pltpu.CompilerParams(
                collective_id=0,
                has_side_effects=True,
                vmem_limit_bytes=16 * 1024 * 1024,
            ),
        )(table)
        return pl.pallas_call(
            finish_kernel,
            out_shape=jax.ShapeDtypeStruct(block, jnp.float32),
            in_specs=[pl.BlockSpec(memory_space=pltpu.VMEM)] * 3,
            out_specs=pl.BlockSpec(memory_space=pl.ANY),
            scratch_shapes=[
                pltpu.VMEM((2, 8, 2048), jnp.float32),
                pltpu.SemaphoreType.DMA((2,)),
            ],
            compiler_params=pltpu.CompilerParams(vmem_limit_bytes=16 * 1024 * 1024),
        )(*parts)

    return jax.shard_map(
        step,
        mesh=mesh,
        in_specs=(P("sx", "sy", "vel"),),
        out_specs=P("sx", "sy", "vel"),
        check_vma=False,
    )
```
